512 devices in a mesh: img: 16 (over z_hi, y, core), term: 32 (over z_lo, x).
Axes of the slice: x: 4, y: 4, z: 16 (z_hi: 2, z_lo: 8; z = z_hi * 8 + z_lo), core: 2. Of those that a mesh axis runs over, the one named last changes fastest.
Arguments:
- patches: bfloat16 [64, 256, 1024], P('img', 'term'), may hold values from -6 to 6
- patch_mask: int32 [64, 256], P('img', 'term'), may hold values 0 or 1
- proj_weight: bfloat16 [1024, 30720], P('img', 'term'), may hold values from -0.1875 to 0.1875
- proj_bias: float32 [30720], P('term'), may hold values from -4 to 4
- slab: bfloat16 [8128, 30720], P('img', 'term'), may hold values from 0 to 2
- query_ids: int32 [1024, 32], replicated, may hold values from -1 to 30719, as said below
- term_weights: bfloat16 [1024, 32], replicated, may hold values from 0.25 to 4
Outputs:
- scores: float32 [1024, 8192], P('term', 'img')
The draws below stay inside these ranges and needn't reach their ends.
Inputs may be any that keep to these rules, and one draw needn't show every extreme that they name: `query_ids`: within a query the non-negative ids are distinct and come before the padding slots; every query has at least 8 real terms and some query fills all 32 slots.
All inputs are finite; a program needn't handle non-finite values. No bound on the sum of `patch_mask` on one device may be relied on, other than what follows from the above.
Results may differ from the reference program's by a relative error of at most 0.0003.
Values may be sent and summed in bfloat16 or wider, within the bound.
A program may use at most 64 MiB of HBM per device.

```python
import math
import jax
import jax.numpy as jnp
from jax import lax

D = 1024
V = 30720
P_SIZE = 256
L = 32
Q = 1024
NEW_DEV = 4
SLAB_DEV = 508
NEW = 64
SLAB = 8128
IMGS = 8192
N_IMG = 16


def draw_query_ids(key, part):
    key_len = jax.random.fold_in(key, 11)
    key_pick = jax.random.fold_in(key, 12)
    key_rank = jax.random.fold_in(key, 13)
    lengths = jax.random.randint(key_len, (Q,), L // 4, L + 1)
    chosen = jax.random.randint(key_pick, (), 0, Q)
    lengths = jnp.where(jnp.arange(Q) == chosen, L, lengths)
    ranking = jax.random.randint(key_rank, (Q, V), 0, 2 ** 30 // V) * V + jnp.arange(V, dtype=jnp.int32)[None, :]
    _, chosen_ids = lax.top_k(ranking, L)
    slots = jnp.arange(L)[None, :]
    return jnp.where(slots < lengths[:, None], chosen_ids, -1).astype(jnp.int32)


def touch_ends(values, stream_key, least, largest):
    longest = values.shape.index(max(values.shape))
    spots = []
    for shift in (0, 1):
        where = [jax.random.randint(jax.random.fold_in(stream_key, axis), (), 0, length) for axis, length in enumerate(values.shape)]
        where[longest] = (where[longest] + shift) % values.shape[longest]
        spots.append(tuple(where))
    return values.at[spots[0]].set(least).at[spots[1]].set(largest)


def shard_levels(rng, shape, split, least, largest):
    gain, own = 1.0, jax.random.fold_in(rng, 6)
    for dim, parts in split:
        heights = jnp.exp(jax.random.uniform(jax.random.fold_in(own, dim), (parts,), jnp.float32, least / len(split), largest / len(split)))
        gain = gain * jnp.repeat(heights, shape[dim] // parts).reshape([-1 if axis == dim else 1 for axis in range(len(shape))])
    return gain


def gaussian(key, shape, scale, reach, pieces=(), kind=jnp.bfloat16):
    values = scale * jax.random.normal(key, shape, jnp.float32)
    if pieces:
        values = values * shard_levels(key, shape, pieces, -0.22, 0.18)
    return jnp.clip(values, -reach, reach).astype(kind)


def setup_inputs(seed: int = 0) -> dict:
    key_of = jax.random.split(jax.random.key(seed), 8)
    return {
        "patches": gaussian(key_of[0], (NEW, P_SIZE, D), 1.0, 6.0, ((0, 16), (1, 32))),
        "patch_mask": touch_ends((jax.random.randint(key_of[1], (NEW, P_SIZE), 0, 4) < 3).astype(jnp.int32), jax.random.fold_in(key_of[1], 1), 0, 1),
        "proj_weight": gaussian(key_of[2], (D, V), D ** -0.5, 0.1875, ((0, 16), (1, 32))),
        "proj_bias": gaussian(key_of[3], (V,), 1.0, 4.0, ((0, 32),), jnp.float32),
        "slab": jnp.clip(2.0 * jax.random.uniform(key_of[4], (SLAB, V), jnp.float32) ** shard_levels(key_of[4], (SLAB, V), ((0, 16), (1, 32)), -0.2, 0.2), 0.0, 2.0).astype(jnp.bfloat16),
        "query_ids": draw_query_ids(jax.random.fold_in(key_of[7], 71), 0),
        "term_weights": jnp.clip(jnp.exp(jax.random.uniform(key_of[6], (Q, L), jnp.float32, math.log(0.25), math.log(4.0))), 0.25, 4.0).astype(jnp.bfloat16),
    }


def one_image(pair, proj_weight, proj_bias):
    features, keep_mask = pair
    logits = jnp.dot(features, proj_weight, preferred_element_type=jnp.float32) + proj_bias
    activity = jnp.log1p(jnp.maximum(logits, 0.0))
    activity = jnp.where(keep_mask[:, None] > 0, activity, 0.0)
    return jnp.max(activity, axis=0)


def reference(patches, patch_mask, proj_weight, proj_bias, slab, query_ids, term_weights):
    new_impacts = lax.map(lambda pair: one_image(pair, proj_weight, proj_bias), (patches, patch_mask))
    new_impacts = new_impacts.astype(jnp.bfloat16)
    impacts = jnp.concatenate([slab.reshape(N_IMG, SLAB_DEV, V), new_impacts.reshape(N_IMG, NEW_DEV, V)], axis=1)
    impacts = impacts.reshape(IMGS, V)
    query_weight = jnp.where(query_ids >= 0, term_weights, jnp.zeros((), jnp.bfloat16)).astype(jnp.bfloat16)
    safe_ids = jnp.maximum(query_ids, 0).astype(jnp.int32)
    blocks = Q // 64 if Q % 64 == 0 else Q
    rows_block = Q // blocks

    def score_block(pair):
        ids_block, weight_block = pair
        picked = jnp.take(impacts, ids_block, axis=1).astype(jnp.float32)
        return jnp.sum(picked * weight_block.astype(jnp.float32)[None], axis=2).T

    result = lax.map(score_block, (safe_ids.reshape(blocks, rows_block, L), query_weight.reshape(blocks, rows_block, L)))
    return result.reshape(Q, IMGS)
```

```python
import functools

import jax
import jax.numpy as jnp
from jax import lax
from jax.experimental import pallas as pl
from jax.experimental.pallas import tpu as pltpu
from jax.sharding import PartitionSpec as P

MESH = pl.DeviceIdType.MESH
NX, NY, NZ, NH = 4, 4, 8, 2
EXTRA = 128
FAR = (4, 3, 5, 2, 6, 1, 7, 0)
MASKED = -1e30


def remote(src, dst, send, recv, **where):
    return pltpu.make_async_remote_copy(
        src_ref=src, dst_ref=dst, send_sem=send, recv_sem=recv, device_id=where, device_id_type=MESH
    )


def kernel(
    ids_ref, tw_ref, bias_ref, pat_ref, wt_ref, slab_ref,
    main_ref, new_ref,
    feats, weight, dense, part, half_in, full_in, z_in, relay, runmax, fresh, fresh_x, fresh_z, fresh_in,
    zs, zr, xs, xr, hs, hr, rs, rr, ws, wr, ys, yr, cs, cr,
    as_, ar, bs, br, qs, qr, tx_s, tx_r, tz_s, tz_r,
):
    img = lax.axis_index("img")
    term = lax.axis_index("term")
    core, y, zh = lax.rem(img, 2), lax.rem(lax.div(img, 2), NY), lax.div(img, 2 * NY)
    x, zl = lax.rem(term, NX), lax.div(term, NX)

    def at_x(d):
        return zl * NX + lax.rem(x + d, NX)

    def at_zl(k):
        return k * NX + x

    def at_y(d):
        return zh * 8 + lax.rem(y + d, NY) * 2 + core

    def at_z(d):
        far = lax.rem(zh * NZ + zl + d, NH * NZ)
        return {"img": lax.div(far, NZ) * 8 + y * 2 + core, "term": lax.rem(far, NZ) * NX + x}

    partner = zh * 8 + y * 2 + 1 - core
    out_of_line = at_z(jnp.where(zl < 4, 12, 4))

    barrier = pltpu.get_barrier_semaphore()
    for d in range(1, NZ):
        pl.semaphore_signal(barrier, inc=1, device_id={"term": at_zl(lax.rem(zl + d, NZ))}, device_id_type=MESH)
    pl.semaphore_signal(barrier, inc=1, device_id=out_of_line, device_id_type=MESH)
    for d in range(1, NX):
        pl.semaphore_signal(barrier, inc=1, device_id={"term": at_x(d)}, device_id_type=MESH)
    for d in range(1, NY):
        pl.semaphore_signal(barrier, inc=1, device_id={"img": at_y(d)}, device_id_type=MESH)
    pl.semaphore_signal(barrier, inc=1, device_id={"img": partner}, device_id_type=MESH)

    width = dense.shape[1]
    first = term * width

    def chunk(k):
        c = lax.rem(zl + FAR[k], NZ)

        def rows16(r, carry):
            rows = pl.ds(pl.multiple_of(c * 128 + r * 16, 16), 16)
            ids = ids_ref[rows, :] - first
            tw = tw_ref[rows, :].astype(jnp.float32)
            lane = lax.broadcasted_iota(jnp.int32, (16, width), 1)
            acc = jnp.zeros((16, width), jnp.float32)
            for j in range(ids.shape[1]):
                acc = jnp.where(ids[:, j : j + 1] == lane, tw[:, j : j + 1], acc)
            dense[rows, :] = acc.astype(jnp.bfloat16)
            return carry

        lax.fori_loop(0, 8, rows16, 0)
        share = lax.dot_general(
            dense[pl.ds(pl.multiple_of(c * 128, 128), 128), :], slab_ref[...],
            (((1,), (1,)), ((), ())), preferred_element_type=jnp.float32,
        )
        stored = slab_ref.shape[0]
        for d in range(NX):
            part[c, d, :, 384:512] = jnp.zeros((32, 128), jnp.float32)
            part[c, d, :, 0:stored] = share[d * 32 : (d + 1) * 32, :]

    chunk(0)
    pl.semaphore_wait(barrier, 15)

    def block(o):
        return pat_ref if o is None else feats.at[x, o]

    def z_right(src, o):
        return remote(src, feats.at[x, o], zs.at[0, o], zr.at[o], term=at_zl(zl + 1))

    def z_left(src, o):
        return remote(src, feats.at[x, o], zs.at[1, o], zr.at[o], term=at_zl(zl - 1))

    def x_send(src, o, way):
        return remote(src, feats.at[x, o], xs.at[way, o], xr.at[way, o], term=at_x((1, 3)[way]))

    def x_forward(o, way):
        owner = lax.rem(x + (3, 1)[way], NX)
        rows = pl.ds(way * 16, 16)
        return remote(
            feats.at[owner, o, rows], feats.at[owner, o, rows], hs.at[way, o], hr.at[way, o], term=at_x((1, 3)[way])
        )

    def x_take(o, way):
        owner = lax.rem(x + (3, 1)[way], NX)
        remote(feats.at[owner, o], feats.at[owner, o], xs.at[way, o], xr.at[way, o], term=at_x((1, 3)[way])).wait_recv()

    def half_take(o, way):
        owner = lax.rem(x + 2, NX)
        rows = pl.ds(way * 16, 16)
        remote(
            feats.at[owner, o, rows], feats.at[owner, o, rows], hs.at[way, o], hr.at[way, o], term=at_x((1, 3)[way])
        ).wait_recv()

    def spread(src, o):
        x_send(src, o, 0).start()
        x_send(src, o, 1).start()

    def pass_on(o):
        for way in (0, 1):
            x_take(o, way)
            x_forward(o, way).start()

    def rows_of(h, yy, cc, lo=0, n=64):
        return weight.at[pl.ds(pl.multiple_of((h * 8 + yy * 2 + cc) * 64 + lo, 32), n)]

    def relay_send(way):
        return remote(wt_ref.at[pl.ds(way * 32, 32)], relay.at[way], rs.at[way], rr.at[way], **at_z((4, 12)[way]))

    def relay_on(way):
        far = at_z((4, 12)[way])
        h = lax.div(far["img"], 8)
        dst = rows_of(1 - h, y, core, way * 32, 32)
        return remote(relay.at[way], dst, ws.at[way], wr.at[way], **far)

    def relay_take(way):
        far = at_z((4, 12)[way])
        dst = rows_of(1 - zh, y, core, way * 32, 32)
        remote(relay.at[way], dst, ws.at[way], wr.at[way], **far).wait_recv()

    def y_send(b, d):
        src = wt_ref if b == 0 else rows_of(1 - zh, y, core)
        h = zh if b == 0 else 1 - zh
        return remote(src, rows_of(h, y, core), ys.at[b, d - 1], yr.at[b, d - 1], img=at_y(d))

    def y_take(b, d):
        h = zh if b == 0 else 1 - zh
        dst = rows_of(h, lax.rem(y + NY - d, NY), core)
        remote(dst, dst, ys.at[b, d - 1], yr.at[b, d - 1], img=at_y(d)).wait_recv()

    def c_send(b, d):
        h = zh if b == 0 else 1 - zh
        dst = rows_of(h, lax.rem(y + NY - d, NY), core)
        src = wt_ref if (b == 0 and d == 0) else dst
        return remote(src, dst, cs.at[b, d], cr.at[b, d], img=partner)

    def c_take(b, d):
        h = zh if b == 0 else 1 - zh
        dst = rows_of(h, lax.rem(y + NY - d, NY), 1 - core)
        remote(dst, dst, cs.at[b, d], cr.at[b, d], img=partner).wait_recv()

    def a_copy(k, way):
        c = lax.rem(zl + FAR[k], NZ)
        src = part.at[c, lax.rem(x + 2, NX), pl.ds(way * 16, 16)]
        return remote(src, half_in.at[k, way], as_.at[k, way], ar.at[k, way], term=at_x((1, 3)[way]))

    def b_copy(k, way):
        c = lax.rem(zl + FAR[k], NZ)
        src = part.at[c, lax.rem(x + (1, 3)[way], NX)]
        return remote(src, full_in.at[k, way], bs.at[k, way], br.at[k, way], term=at_x((1, 3)[way]))

    def q_copy(k):
        c = lax.rem(zl + FAR[k], NZ)
        return remote(part.at[c, x], z_in.at[k], qs.at[k], qr.at[k], term=at_zl(c))

    def stage_a(k):
        for way in (0, 1):
            a_copy(k, way).start()

    def stage_b(k):
        c = lax.rem(zl + FAR[k], NZ)
        for way in (0, 1):
            a_copy(k, way).wait_recv()
            to = lax.rem(x + (1, 3)[way], NX)
            rows = slice(way * 16, way * 16 + 16)
            part[c, to, rows, :] = part[c, to, rows, :] + half_in[k, way]
            b_copy(k, way).start()

    def stage_c(k):
        c = lax.rem(zl + FAR[k], NZ)
        for way in (0, 1):
            b_copy(k, way).wait_recv()
        part[c, x] = part[c, x] + (full_in[k, 0] + full_in[k, 1])
        if FAR[k]:
            q_copy(k).start()

    @pl.when(zl < NZ - 1)
    def _():
        z_right(pat_ref, zl).start()

    @pl.when(zl > 0)
    def _():
        z_left(pat_ref, zl).start()

    for way in (0, 1):
        relay_send(way).start()
    spread(pat_ref, zl)
    for d in range(1, NY):
        y_send(0, d).start()
    c_send(0, 0).start()
    stage_a(0)

    feats[x, zl] = pat_ref[...]
    weight[pl.ds(pl.multiple_of(img * 64, 64), 64), :] = wt_ref[...]
    depth = weight.shape[0] - EXTRA
    top = lax.broadcasted_iota(jnp.int32, (EXTRA, width), 0) == 0
    weight[depth:, :] = jnp.where(top, MASKED, 0.0).astype(jnp.bfloat16)

    for s in range(1, NZ):
        if s == 1:
            pass_on(zl)
        else:
            @pl.when(zl >= s - 1)
            def _():
                pass_on(zl - (s - 1))

            @pl.when(zl + s - 1 < NZ)
            def _():
                pass_on(zl + s - 1)

        @pl.when(zl >= s)
        def _():
            o = zl - s
            remote(feats.at[x, o], feats.at[x, o], zs.at[0, o], zr.at[o], term=at_x(1)).wait_recv()

            @pl.when(zl < NZ - 1)
            def _():
                z_right(feats.at[x, o], o).start()

            spread(feats.at[x, o], o)

        @pl.when(zl + s < NZ)
        def _():
            o = zl + s
            remote(feats.at[x, o], feats.at[x, o], zs.at[1, o], zr.at[o], term=at_x(1)).wait_recv()

            @pl.when(zl > 0)
            def _():
                z_left(feats.at[x, o], o).start()

            spread(feats.at[x, o], o)

        if s == 2:
            for way in (0, 1):
                relay_send(way).wait_recv()
                relay_on(way).start()
        if s == 4:
            for way in (0, 1):
                relay_take(way)
            for d in range(1, NY):
                y_send(1, d).start()
            c_send(1, 0).start()
        if s in (3, 5, 6):
            d = {3: 1, 5: 2, 6: 3}[s]
            y_take(0, d)
            c_send(0, d).start()
        chunk(s)
        stage_a(s)
        stage_b(s - 1)
        if s >= 2:
            stage_c(s - 2)

    @pl.when(zl >= NZ - 1)
    def _():
        pass_on(0)

    @pl.when(zl <= 0)
    def _():
        pass_on(NZ - 1)

    for d in range(1, NY):
        y_take(1, d)
        c_send(1, d).start()
    stage_b(NZ - 1)
    stage_c(NZ - 2)
    for b in (0, 1):
        for d in range(NY):
            c_take(b, d)
    for o in range(NZ):
        for way in (0, 1):
            half_take(o, way)

    runmax[...] = jnp.full(runmax.shape, MASKED, jnp.float32)

    def group(g, carry):
        rows = feats[g].reshape(NZ * 32, feats.shape[3])
        logits = jnp.dot(rows, weight[...], preferred_element_type=jnp.float32)
        runmax[...] = jnp.maximum(runmax[...], jnp.max(logits.reshape(NZ, 32, width), axis=0))
        return carry

    lax.fori_loop(0, NX, group, 0)
    best = jnp.max(runmax[...].reshape(4, 8, width), axis=1)
    best = jnp.log1p(jnp.maximum(best + bias_ref[...], 0.0)).astype(jnp.bfloat16)
    best = jnp.concatenate([best, jnp.zeros_like(best)], axis=0)
    fresh[...] = lax.dot_general(
        best, dense[...], (((1,), (1,)), ((), ())), preferred_element_type=jnp.float32
    )

    def tx_copy(d):
        return remote(fresh, fresh_x.at[d - 1], tx_s.at[d - 1], tx_r.at[d - 1], term=at_x(d))

    def tz_copy(d):
        to = lax.rem(zl + d, NZ)
        return remote(fresh_z.at[to], fresh_in.at[d - 1], tz_s.at[d - 1], tz_r.at[d - 1], term=at_zl(to))

    for d in range(1, NX):
        tx_copy(d).start()
    stage_c(NZ - 1)
    for d in range(1, NX):
        tx_copy(d).wait_recv()
    total = fresh[...] + fresh_x[0] + fresh_x[1] + fresh_x[2]
    for k in range(NZ):
        fresh_z[k] = total[:, k * 128 : (k + 1) * 128]
    for d in range(1, NZ):
        tz_copy(d).start()
    result = part[zl, x]
    for k in range(NZ - 1):
        q_copy(k).wait_recv()
        result = result + z_in[k]
    main_ref[...] = result
    total = fresh_z[zl]
    for d in range(1, NZ):
        tz_copy(d).wait_recv()
        total = total + fresh_in[d - 1]
    new_ref[...] = total

    for o in range(NZ):
        @pl.when(jnp.logical_and(zl < NZ - 1, o <= zl))
        def _():
            z_right(feats.at[x, o], o).wait_send()

        @pl.when(jnp.logical_and(zl > 0, o >= zl))
        def _():
            z_left(feats.at[x, o], o).wait_send()

        for way in (0, 1):
            x_send(feats.at[x, o], o, way).wait_send()
            x_forward(o, way).wait_send()
    for way in (0, 1):
        relay_send(way).wait_send()
        relay_on(way).wait_send()
    for b in (0, 1):
        for d in range(1, NY):
            y_send(b, d).wait_send()
        for d in range(NY):
            c_send(b, d).wait_send()
    for k in range(NZ):
        for way in (0, 1):
            a_copy(k, way).wait_send()
            b_copy(k, way).wait_send()
        if FAR[k]:
            q_copy(k).wait_send()
    for d in range(1, NX):
        tx_copy(d).wait_send()
    for d in range(1, NZ):
        tz_copy(d).wait_send()


def shards(patches, patch_mask, proj_weight, proj_bias, slab, query_ids, term_weights):
    images, chunk, depth = patches.shape
    rows = images * chunk
    width = proj_weight.shape[1]
    masked = (1 - patch_mask.reshape(rows, 1)).astype(jnp.bfloat16)
    block = jnp.concatenate(
        [patches.reshape(rows, depth), jnp.pad(masked, ((0, 0), (0, EXTRA - 1)))], axis=1
    )
    queries = query_ids.shape[0]
    f32, b16 = jnp.float32, jnp.bfloat16
    dma = pltpu.SemaphoreType.DMA
    vmem = pl.BlockSpec(memory_space=pltpu.VMEM)
    main, new = pl.pallas_call(
        kernel,
        out_shape=(jax.ShapeDtypeStruct((32, 512), f32), jax.ShapeDtypeStruct((8, 128), f32)),
        in_specs=[vmem] * 6,
        out_specs=(vmem, vmem),
        scratch_shapes=[
            pltpu.VMEM((NX, NZ, rows, depth + EXTRA), b16),
            pltpu.VMEM((depth + EXTRA, width), b16),
            pltpu.VMEM((queries, width), b16),
            pltpu.VMEM((NZ, NX, 32, 512), f32),
            pltpu.VMEM((NZ, 2, 16, 512), f32),
            pltpu.VMEM((NZ, 2, 32, 512), f32),
            pltpu.VMEM((NZ - 1, 32, 512), f32),
            pltpu.VMEM((2, 32, width), b16),
            pltpu.VMEM((rows, width), f32),
            pltpu.VMEM((8, queries), f32),
            pltpu.VMEM((NX - 1, 8, queries), f32),
            pltpu.VMEM((NZ, 8, 128), f32),
            pltpu.VMEM((NZ - 1, 8, 128), f32),
            dma((2, NZ)), dma((NZ,)), dma((2, NZ)), dma((2, NZ)), dma((2, NZ)), dma((2, NZ)),
            dma((2,)), dma((2,)), dma((2,)), dma((2,)),
            dma((2, NY - 1)), dma((2, NY - 1)), dma((2, NY)), dma((2, NY)),
            dma((NZ, 2)), dma((NZ, 2)), dma((NZ, 2)), dma((NZ, 2)), dma((NZ - 1,)), dma((NZ - 1,)),
            dma((NX - 1,)), dma((NX - 1,)), dma((NZ - 1,)), dma((NZ - 1,)),
        ],
        compiler_params=pltpu.CompilerParams(
            collective_id=0, has_side_effects=True, vmem_limit_bytes=60 * 1024 * 1024
        ),
        name="score",
    )(query_ids, term_weights, proj_bias.reshape(1, width), block, proj_weight, slab)
    mine = lax.rem(lax.axis_index("term"), NX)
    new = lax.dynamic_slice(new, (0, mine * 32), (images, 32))
    return jnp.concatenate([main[:, : slab.shape[0]], new.T], axis=1)


def solution(mesh):
    placed = (
        P("img", "term", None),
        P("img", "term"),
        P("img", "term"),
        P("term"),
        P("img", "term"),
        P(),
        P(),
    )
    return jax.shard_map(
        shards, mesh=mesh, in_specs=placed, out_specs=P("term", "img"), check_vma=False
    )
```

```python
import functools

import jax
import jax.numpy as jnp
from jax import lax
from jax.experimental import pallas as pl
from jax.experimental.pallas import tpu as pltpu
from jax.sharding import PartitionSpec as P

MESH = pl.DeviceIdType.MESH
NX, NY, NZ, NH = 4, 4, 8, 2
EXTRA = 128
FAR = (4, 3, 5, 2, 6, 1, 7, 0)
ONWARD = {0: (1,), 1: (1,), 2: (1,), 3: (1,), 4: (1,), 5: (1,), 6: (1,)}
MASKED = -1e30
PLAN = (
    ("chunk", 1), ("shares", 0), ("arrive", 1), ("chunk", 2), ("shares", 1), ("relay",), ("pass", 0),
    ("arrive", 2), ("chunk", 3), ("shares", 2), ("pass", 1), ("arrive", 3), ("chunk", 4), ("shares", 3),
    ("pass", 2), ("arrive", 4), ("chunk", 5), ("other",), ("row", 1), ("row", 2), ("row", 3), ("pass", 3),
    ("arrive", 5), ("chunk", 6), ("pass", 4), ("arrive", 6), ("chunk", 7), ("pass", 5), ("arrive", 7),
    ("row2", 1), ("row2", 2), ("row2", 3), ("pass", 6), ("pass", 7), ("shares", 4), ("shares", 5),
    ("shares", 6), ("shares", 7), ("gather", 0), ("gather", 1), ("rows",), ("project", 0), ("project", 1),
    ("project", 3), ("project", 2), ("new",), ("gather", 2), ("gather", 3), ("gather", 4), ("new2",),
    ("gather", 5), ("gather", 6), ("gather", 7),
)


def remote(src, dst, send, recv, **where):
    return pltpu.make_async_remote_copy(
        src_ref=src, dst_ref=dst, send_sem=send, recv_sem=recv, device_id=where, device_id_type=MESH
    )


def kernel(
    ids_ref, tw_ref, mask_ref, bias_ref, pat_ref, wt_ref, slab_ref,
    out_ref,
    ids_v, tw_v, slab_v, tile_ids, tile_tw, feats, weight, dense, part, x_out, x_in, z_out, z_in, relay, runmax,
    fresh, fresh_x, fresh_z, fresh_in, turned,
    ls, zs, zr, xs, xr, hs, hr, rs, rr, ws, wr, ys, yr, cs, cr,
    as_, ar, qs, qr, tx_s, tx_r, tz_s, tz_r,
):
    img = lax.axis_index("img")
    term = lax.axis_index("term")
    core, y, zh = lax.rem(img, 2), lax.rem(lax.div(img, 2), NY), lax.div(img, 2 * NY)
    x, zl = lax.rem(term, NX), lax.div(term, NX)
    depth = weight.shape[0] - EXTRA
    width = weight.shape[1]
    stored = slab_v.shape[1]

    def at_x(d):
        return zl * NX + lax.rem(x + d, NX)

    def at_zl(k):
        return k * NX + x

    def at_y(d):
        return zh * 8 + lax.rem(y + d, NY) * 2 + core

    def at_z(d):
        far = lax.rem(zh * NZ + zl + d, NH * NZ)
        return {"img": lax.div(far, NZ) * 8 + y * 2 + core, "term": lax.rem(far, NZ) * NX + x}

    partner = zh * 8 + y * 2 + 1 - core

    barrier = pltpu.get_barrier_semaphore()
    for hop in (4, 2, 1):
        for to in (zl + hop, zl - hop):
            @pl.when(jnp.logical_and(to >= 0, to < NZ))
            def _():
                pl.semaphore_signal(barrier, inc=1, device_id={"term": at_zl(to)}, device_id_type=MESH)
    pl.semaphore_signal(barrier, inc=1, device_id=at_z(jnp.where(zl < 4, 12, 4)), device_id_type=MESH)
    for d in range(1, NX):
        pl.semaphore_signal(barrier, inc=1, device_id={"term": at_x(d)}, device_id_type=MESH)
    for d in range(1, NY):
        pl.semaphore_signal(barrier, inc=1, device_id={"img": at_y(d)}, device_id_type=MESH)
    pl.semaphore_signal(barrier, inc=1, device_id={"img": partner}, device_id_type=MESH)
    near = 1 + jnp.where(jnp.logical_or(zl == 0, zl == NZ - 1), 1, 2) + jnp.where(
        jnp.logical_or(zl < 2, zl >= NZ - 2), 1, 2
    )

    own = weight.at[pl.ds(pl.multiple_of(img * 64, 64), 64)]
    local = [
        pltpu.make_async_copy(ids_ref, ids_v, ls.at[0]),
        pltpu.make_async_copy(tw_ref, tw_v, ls.at[1]),
        pltpu.make_async_copy(pat_ref, feats.at[x, zl, :, pl.ds(0, depth)], ls.at[2]),
        pltpu.make_async_copy(wt_ref, own, ls.at[3]),
        pltpu.make_async_copy(slab_ref, slab_v, ls.at[4]),
    ]
    for copy in local:
        copy.start()

    square = lax.broadcasted_iota(jnp.int32, (8, 8), 0) == lax.broadcasted_iota(jnp.int32, (8, 8), 1)
    off = []
    for n in range(mask_ref.shape[0]):
        row = jnp.broadcast_to(mask_ref[n : n + 1, :], (8, 8)).astype(jnp.float32)
        off.append(1.0 - jnp.sum(jnp.where(square, row, 0.0), axis=1, keepdims=True))
    off = jnp.concatenate(off, axis=0)
    lane = lax.broadcasted_iota(jnp.int32, (off.shape[0], EXTRA), 1)
    feats[x, zl, :, depth:] = jnp.where(lane == 0, off, 0.0).astype(jnp.bfloat16)
    top = lax.broadcasted_iota(jnp.int32, (EXTRA, width), 0) == 0
    weight[depth:, :] = jnp.where(top, MASKED, 0.0).astype(jnp.bfloat16)

    first = term * width
    local[0].wait()
    local[1].wait()

    def chunk(k):
        c = lax.rem(zl + FAR[k], NZ)
        slots = ids_v.shape[0]
        ids = (ids_v[:, pl.ds(pl.multiple_of(c * 128, 128), 128)] - first).astype(jnp.int16)
        tw = tw_v[:, pl.ds(pl.multiple_of(c * 128, 128), 128)]
        for j in range(slots):
            tile_ids[j] = jnp.broadcast_to(ids[j : j + 1, :], (16, 128))
            tile_tw[j] = jnp.broadcast_to(tw[j : j + 1, :], (16, 128))

        def band(r, carry):
            shape = (15, 16, 128)
            term_of = (
                lax.broadcasted_iota(jnp.int32, shape, 0) * 16 + lax.broadcasted_iota(jnp.int32, shape, 1) + r * 240
            ).astype(jnp.int16)
            acc = jnp.zeros(shape, jnp.bfloat16)
            for j in range(slots):
                acc = jnp.where(tile_ids[j][None] == term_of, tile_tw[j][None], acc)
            dense[c, pl.ds(pl.multiple_of(r * 240, 240), 240), :] = acc.reshape(240, 128)
            return carry

        lax.fori_loop(0, width // 240, band, 0)
        if k == 0:
            local[4].wait()
        share = lax.dot_general(
            dense[c], slab_v[...], (((0,), (0,)), ((), ())), preferred_element_type=jnp.float32
        )
        for d in range(NX):
            part[c, d, :, 384:512] = jnp.zeros((32, 128), jnp.float32)
            part[c, d, :, 0:stored] = share[d * 32 : (d + 1) * 32, :]

    chunk(0)
    local[2].wait()
    local[3].wait()
    pl.semaphore_wait(barrier, near + 8)

    def half(owner, o, h):
        return feats.at[owner, o, pl.ds(h * 16, 16)]

    def z_send(o, way, hop, h):
        to = zl + hop if way == 0 else zl - hop
        return remote(half(x, o, h), half(x, o, h), zs.at[way, o, hop // 2, h], zr.at[o, h], term=at_zl(to))

    def z_onward(o, k, way, h, finish=False):
        for hop in ONWARD.get(k, ()):
            @pl.when(zl + hop < NZ if way == 0 else zl >= hop)
            def _():
                copy = z_send(o, way, hop, h)
                copy.wait_send() if finish else copy.start()

    def x_send(o, way, h):
        return remote(half(x, o, h), half(x, o, h), xs.at[way, o, h], xr.at[way, o, h], term=at_x((1, 3)[way]))

    def x_forward(o, way):
        rows = half(lax.rem(x + (3, 1)[way], NX), o, way)
        return remote(rows, rows, hs.at[way, o], hr.at[way, o], term=at_x((1, 3)[way]))

    def x_take(o, way, h):
        rows = half(lax.rem(x + (3, 1)[way], NX), o, h)
        remote(rows, rows, xs.at[way, o, h], xr.at[way, o, h], term=at_x((1, 3)[way])).wait_recv()

    def half_take(o, way):
        rows = half(lax.rem(x + 2, NX), o, way)
        remote(rows, rows, hs.at[way, o], hr.at[way, o], term=at_x((1, 3)[way])).wait_recv()

    def sides(k, act):
        @pl.when(zl >= k)
        def _():
            act(zl - k, 0)

        @pl.when(zl + k < NZ)
        def _():
            act(zl + k, 1)

    def arrive(k):
        def act(o, way):
            for h in (0, 1):
                z_send(o, way, 1, h).wait_recv()
                z_onward(o, k, way, h)
                x_send(o, h, h).start()
                x_send(o, 1 - h, h).start()

        sides(k, act)

    def pass_on(k):
        def act(o, way):
            for turn in (0, 1):
                x_take(o, turn, turn)
                x_forward(o, turn).start()

        act(zl, 0) if k == 0 else sides(k, act)

    def rows_of(h, yy, cc, lo=0, n=64):
        return weight.at[pl.ds(pl.multiple_of((h * 8 + yy * 2 + cc) * 64 + lo, 32), n)]

    def relay_send(way):
        return remote(rows_of(zh, y, core, way * 32, 32), relay.at[way], rs.at[way], rr.at[way], **at_z((4, 12)[way]))

    def relay_on(way):
        far = at_z((4, 12)[way])
        h = lax.div(far["img"], 8)
        dst = rows_of(1 - h, y, core, way * 32, 32)
        return remote(relay.at[way], dst, ws.at[way], wr.at[way], **far)

    def relay_take(way):
        far = at_z((4, 12)[way])
        dst = rows_of(1 - zh, y, core, way * 32, 32)
        remote(relay.at[way], dst, ws.at[way], wr.at[way], **far).wait_recv()

    def y_send(b, d):
        rows = rows_of(zh if b == 0 else 1 - zh, y, core)
        return remote(rows, rows, ys.at[b, d - 1], yr.at[b, d - 1], img=at_y(d))

    def y_take(b, d):
        h = zh if b == 0 else 1 - zh
        dst = rows_of(h, lax.rem(y + NY - d, NY), core)
        remote(dst, dst, ys.at[b, d - 1], yr.at[b, d - 1], img=at_y(d)).wait_recv()

    def c_send(b, d):
        h = zh if b == 0 else 1 - zh
        rows = rows_of(h, lax.rem(y + NY - d, NY), core)
        return remote(rows, rows, cs.at[b, d], cr.at[b, d], img=partner)

    def c_take(b, d):
        h = zh if b == 0 else 1 - zh
        dst = rows_of(h, lax.rem(y + NY - d, NY), 1 - core)
        remote(dst, dst, cs.at[b, d], cr.at[b, d], img=partner).wait_recv()

    pos = lax.broadcasted_iota(jnp.int32, (32, 512), 1)

    def encode(v):
        v = jnp.where(pos < stored, v, 0.0)
        top = jnp.max(v, axis=1, keepdims=True)
        power = jnp.ceil(jnp.log2(jnp.maximum(top, 2.0**-100)))
        code = jnp.minimum((v * (jnp.exp2(-power) * 65535.0) + 0.5).astype(jnp.int32), 65535) - 32768
        return jnp.where(pos == stored, power.astype(jnp.int32), code).astype(jnp.int16)

    def decode(code):
        code = code.astype(jnp.int32)
        step = jnp.exp2(code[:, stored : stored + 1].astype(jnp.float32)) * (1.0 / 65535.0)
        return (code + 32768).astype(jnp.float32) * step

    def share_copy(k, d):
        return remote(x_out.at[k, d - 1], x_in.at[k, d - 1], as_.at[k, d - 1], ar.at[k, d - 1], term=at_x(d))

    def q_copy(k):
        c = lax.rem(zl + FAR[k], NZ)
        return remote(z_out.at[k], z_in.at[k], qs.at[k], qr.at[k], term=at_zl(c))

    def shares(k):
        c = lax.rem(zl + FAR[k], NZ)
        for d in (2, 1, 3):
            x_out[k, d - 1] = encode(part[c, lax.rem(x + d, NX)])
            share_copy(k, d).start()

    def gather_shares(k):
        c = lax.rem(zl + FAR[k], NZ)
        total = part[c, x]
        for d in range(1, NX):
            share_copy(k, d).wait_recv()
            total = total + decode(x_in[k, d - 1])
        if FAR[k]:
            z_out[k] = encode(total)
            q_copy(k).start()
        else:
            part[c, x] = total

    for way in (0, 1):
        relay_send(way).start()
    for h in (0, 1):
        for way in (0, 1):
            z_onward(zl, 0, way, h)
    for h in (0, 1):
        x_send(zl, h, h).start()
        x_send(zl, 1 - h, h).start()
    for d in range(1, NY):
        y_send(0, d).start()
    c_send(0, 0).start()

    def relayed():
        for way in (0, 1):
            relay_send(way).wait_recv()
            relay_on(way).start()

    def other_half():
        for way in (0, 1):
            relay_take(way)
        for d in range(1, NY):
            y_send(1, d).start()
        c_send(1, 0).start()

    def to_partner(b, d):
        y_take(b, d)
        c_send(b, d).start()

    def project(d):
        for o in range(NZ):
            if d == 2:
                half_take(o, 0)
                half_take(o, 1)
            elif d == 3:
                x_take(o, 0, 1)
            elif d == 1:
                x_take(o, 1, 0)
        rows = feats[lax.rem(x + d, NX)].reshape(NZ * 32, feats.shape[3])
        logits = jnp.dot(rows, weight[...], preferred_element_type=jnp.float32)
        best = jnp.max(logits.reshape(NZ, 32, width), axis=0)
        runmax[...] = best if d == 0 else jnp.maximum(runmax[...], best)

    def impacts():
        best = jnp.max(runmax[...].reshape(4, 8, width), axis=1)
        best = jnp.log1p(jnp.maximum(best + bias_ref[...], 0.0)).astype(jnp.bfloat16)
        best = jnp.concatenate([best, jnp.zeros_like(best)], axis=0)
        for k in range(NZ):
            fresh[k] = jnp.dot(best, dense[k], preferred_element_type=jnp.float32)
        for d in range(1, NX):
            tx_copy(d).start()

    def tx_copy(d):
        return remote(fresh, fresh_x.at[d - 1], tx_s.at[d - 1], tx_r.at[d - 1], term=at_x(d))

    def tz_copy(d):
        to = lax.rem(zl + d, NZ)
        return remote(fresh_z.at[to], fresh_in.at[d - 1], tz_s.at[d - 1], tz_r.at[d - 1], term=at_zl(to))

    def out_along_z():
        for d in range(1, NX):
            tx_copy(d).wait_recv()
        fresh_z[...] = fresh[...] + (fresh_x[0] + fresh_x[1] + fresh_x[2])
        for d in range(1, NZ):
            tz_copy(d).start()

    def rows_there():
        for b in (0, 1):
            for d in range(NY):
                c_take(b, d)

    acts = {
        "arrive": arrive, "pass": pass_on, "relay": relayed, "other": other_half,
        "row": lambda d: to_partner(0, d), "row2": lambda d: to_partner(1, d),
        "chunk": chunk, "shares": shares, "gather": gather_shares, "rows": rows_there, "project": project,
        "new": impacts, "new2": out_along_z,
    }
    for name, *at in PLAN:
        acts[name](*at)
    for k in ONWARD:
        for h in (0, 1):
            if k == 0:
                z_onward(zl, 0, 0, h, True)
                z_onward(zl, 0, 1, h, True)
            else:
                sides(k, lambda o, way: z_onward(o, k, way, h, True))
    for o in range(NZ):
        for way in (0, 1):
            x_send(o, way, 0).wait_send()
            x_send(o, way, 1).wait_send()
            x_forward(o, way).wait_send()
    for way in (0, 1):
        relay_send(way).wait_send()
        relay_on(way).wait_send()
    for b in (0, 1):
        for d in range(1, NY):
            y_send(b, d).wait_send()
        for d in range(NY):
            c_send(b, d).wait_send()
    for k in range(NZ):
        for d in range(1, NX):
            share_copy(k, d).wait_send()
        if FAR[k]:
            q_copy(k).wait_send()
    for d in range(1, NX):
        tx_copy(d).wait_send()
    for d in range(1, NZ):
        tz_copy(d).wait_send()

    result = part[zl, x]
    for k in range(NZ - 1):
        q_copy(k).wait_recv()
        result = result + decode(z_in[k])
    out_ref[...] = result

    total = fresh_z[zl]
    for d in range(1, NZ):
        tz_copy(d).wait_recv()
        total = total + fresh_in[d - 1]
    turned[...] = jnp.concatenate([total, jnp.zeros((120, 128), jnp.float32)], axis=0).T
    mine = pltpu.roll(turned[pl.ds(pl.multiple_of(x * 32, 32), 32), :], stored % 128, 1)
    lane = lax.broadcasted_iota(jnp.int32, (32, 128), 1)
    last = out_ref[:, 384:512]
    out_ref[:, 384:512] = jnp.where(lane >= stored % 128, mine, last)


def shards(patches, patch_mask, proj_weight, proj_bias, slab, query_ids, term_weights):
    images, chunk, depth = patches.shape
    rows = images * chunk
    width = proj_weight.shape[1]
    queries, slots = query_ids.shape
    stored = slab.shape[0]
    f32, b16, i16 = jnp.float32, jnp.bfloat16, jnp.int16
    dma = pltpu.SemaphoreType.DMA
    vmem = pl.BlockSpec(memory_space=pltpu.VMEM)
    hbm = pl.BlockSpec(memory_space=pl.ANY)
    return pl.pallas_call(
        kernel,
        out_shape=jax.ShapeDtypeStruct((32, 512), f32),
        in_specs=[hbm, hbm, vmem, vmem, hbm, hbm, hbm],
        out_specs=vmem,
        scratch_shapes=[
            pltpu.VMEM((slots, queries), jnp.int32),
            pltpu.VMEM((slots, queries), b16),
            pltpu.VMEM((width, stored), b16),
            pltpu.VMEM((slots, 16, 128), i16),
            pltpu.VMEM((slots, 16, 128), b16),
            pltpu.VMEM((NX, NZ, rows, depth + EXTRA), b16),
            pltpu.VMEM((depth + EXTRA, width), b16),
            pltpu.VMEM((NZ, width, 128), b16),
            pltpu.VMEM((NZ, NX, 32, 512), f32),
            pltpu.VMEM((NZ, NX - 1, 32, 512), i16),
            pltpu.VMEM((NZ, NX - 1, 32, 512), i16),
            pltpu.VMEM((NZ - 1, 32, 512), i16),
            pltpu.VMEM((NZ - 1, 32, 512), i16),
            pltpu.VMEM((2, 32, width), b16),
            pltpu.VMEM((rows, width), f32),
            pltpu.VMEM((NZ, 8, 128), f32),
            pltpu.VMEM((NX - 1, NZ, 8, 128), f32),
            pltpu.VMEM((NZ, 8, 128), f32),
            pltpu.VMEM((NZ - 1, 8, 128), f32),
            pltpu.VMEM((128, 128), f32),
            dma((5,)),
            dma((2, NZ, 3, 2)), dma((NZ, 2)), dma((2, NZ, 2)), dma((2, NZ, 2)), dma((2, NZ)), dma((2, NZ)),
            dma((2,)), dma((2,)), dma((2,)), dma((2,)),
            dma((2, NY - 1)), dma((2, NY - 1)), dma((2, NY)), dma((2, NY)),
            dma((NZ, NX - 1)), dma((NZ, NX - 1)), dma((NZ - 1,)), dma((NZ - 1,)),
            dma((NX - 1,)), dma((NX - 1,)), dma((NZ - 1,)), dma((NZ - 1,)),
        ],
        compiler_params=pltpu.CompilerParams(
            collective_id=0, has_side_effects=True, vmem_limit_bytes=60 * 1024 * 1024
        ),
        name="score",
    )(
        query_ids.T, term_weights.T, patch_mask, proj_bias.reshape(1, width), patches.reshape(rows, depth),
        proj_weight, slab.T,
    )


def solution(mesh):
    placed = (
        P("img", "term", None),
        P("img", "term"),
        P("img", "term"),
        P("term"),
        P("img", "term"),
        P(),
        P(),
    )
    return jax.shard_map(
        shards, mesh=mesh, in_specs=placed, out_specs=P("term", "img"), check_vma=False
    )
```

```python
import functools

import jax
import jax.numpy as jnp
from jax import lax
from jax.experimental import pallas as pl
from jax.experimental.pallas import tpu as pltpu
from jax.sharding import PartitionSpec as P

MESH = pl.DeviceIdType.MESH
NX, NY, NZ, NH = 4, 4, 8, 2
EXTRA = 128
FAR = (4, 3, 5, 2, 6, 1, 7, 0)
ONWARD = {0: (1,), 1: (1,), 2: (1,), 3: (1,), 4: (1,), 5: (1,), 6: (1,)}
MASKED = -1e30
PLAN = (
    ("chunk", 1), ("shares", 0), ("chunk", 2), ("shares", 1), ("chunk", 3), ("shares", 2), ("chunk", 4),
    ("shares", 3), ("arrive", 1), ("relay",), ("pass", 0), ("chunk", 5), ("shares", 4), ("arrive", 2),
    ("chunk", 6), ("shares", 5), ("pass", 1), ("arrive", 3), ("chunk", 7), ("shares", 6), ("shares", 7),
    ("pass", 2), ("arrive", 4), ("other",), ("row", 1), ("row", 2), ("row", 3), ("arrive", 5), ("pass", 3),
    ("arrive", 6), ("pass", 4), ("arrive", 7), ("pass", 5), ("row2", 1), ("row2", 2), ("row2", 3),
    ("pass", 6), ("gather", 0), ("gather", 1), ("pass", 7), ("gather", 2), ("rows",), ("project", 0),
    ("project", 1), ("gather", 3), ("project", 3), ("project", 2), ("new",), ("gather", 4), ("gather", 5),
    ("new2",), ("gather", 6), ("gather", 7),
)


def remote(src, dst, send, recv, **where):
    return pltpu.make_async_remote_copy(
        src_ref=src, dst_ref=dst, send_sem=send, recv_sem=recv, device_id=where, device_id_type=MESH
    )


def kernel(
    ids_ref, tw_ref, mask_ref, bias_ref, pat_ref, wt_ref, slab_ref,
    out_ref,
    ids_v, tw_v, slab_v, tile_ids, tile_tw, feats, weight, dense, part, x_out, x_in, z_out, z_in, relay, runmax,
    fresh, fresh_x, fresh_z, fresh_in, turned,
    ls, zs, zr, xs, xr, hs, hr, rs, rr, ws, wr, ys, yr, cs, cr,
    as_, ar, qs, qr, tx_s, tx_r, tz_s, tz_r,
):
    img = lax.axis_index("img")
    term = lax.axis_index("term")
    core, y, zh = lax.rem(img, 2), lax.rem(lax.div(img, 2), NY), lax.div(img, 2 * NY)
    x, zl = lax.rem(term, NX), lax.div(term, NX)
    depth = weight.shape[0] - EXTRA
    width = weight.shape[1]
    stored = slab_v.shape[1]

    def at_x(d):
        return zl * NX + lax.rem(x + d, NX)

    def at_zl(k):
        return k * NX + x

    def at_y(d):
        return zh * 8 + lax.rem(y + d, NY) * 2 + core

    def at_z(d):
        far = lax.rem(zh * NZ + zl + d, NH * NZ)
        return {"img": lax.div(far, NZ) * 8 + y * 2 + core, "term": lax.rem(far, NZ) * NX + x}

    partner = zh * 8 + y * 2 + 1 - core

    barrier = pltpu.get_barrier_semaphore()
    for hop in (4, 2, 1):
        for to in (zl + hop, zl - hop):
            @pl.when(jnp.logical_and(to >= 0, to < NZ))
            def _():
                pl.semaphore_signal(barrier, inc=1, device_id={"term": at_zl(to)}, device_id_type=MESH)
    pl.semaphore_signal(barrier, inc=1, device_id=at_z(jnp.where(zl < 4, 12, 4)), device_id_type=MESH)
    for d in range(1, NX):
        pl.semaphore_signal(barrier, inc=1, device_id={"term": at_x(d)}, device_id_type=MESH)
    for d in range(1, NY):
        pl.semaphore_signal(barrier, inc=1, device_id={"img": at_y(d)}, device_id_type=MESH)
    pl.semaphore_signal(barrier, inc=1, device_id={"img": partner}, device_id_type=MESH)
    near = 1 + jnp.where(jnp.logical_or(zl == 0, zl == NZ - 1), 1, 2) + jnp.where(
        jnp.logical_or(zl < 2, zl >= NZ - 2), 1, 2
    )

    own = weight.at[pl.ds(pl.multiple_of(img * 64, 64), 64)]
    local = [
        pltpu.make_async_copy(ids_ref, ids_v, ls.at[0]),
        pltpu.make_async_copy(tw_ref, tw_v, ls.at[1]),
        pltpu.make_async_copy(pat_ref, feats.at[x, zl, :, pl.ds(0, depth)], ls.at[2]),
        pltpu.make_async_copy(wt_ref, own, ls.at[3]),
        pltpu.make_async_copy(slab_ref, slab_v, ls.at[4]),
    ]
    for copy in local:
        copy.start()

    square = lax.broadcasted_iota(jnp.int32, (8, 8), 0) == lax.broadcasted_iota(jnp.int32, (8, 8), 1)
    off = []
    for n in range(mask_ref.shape[0]):
        row = jnp.broadcast_to(mask_ref[n : n + 1, :], (8, 8)).astype(jnp.float32)
        off.append(1.0 - jnp.sum(jnp.where(square, row, 0.0), axis=1, keepdims=True))
    off = jnp.concatenate(off, axis=0)
    lane = lax.broadcasted_iota(jnp.int32, (off.shape[0], EXTRA), 1)
    feats[x, zl, :, depth:] = jnp.where(lane == 0, off, 0.0).astype(jnp.bfloat16)
    top = lax.broadcasted_iota(jnp.int32, (EXTRA, width), 0) == 0
    weight[depth:, :] = jnp.where(top, MASKED, 0.0).astype(jnp.bfloat16)

    first = term * width
    local[0].wait()
    local[1].wait()

    def chunk(k):
        c = lax.rem(zl + FAR[k], NZ)
        slots = ids_v.shape[0]
        ids = (ids_v[:, pl.ds(pl.multiple_of(c * 128, 128), 128)] - first).astype(jnp.int16)
        tw = tw_v[:, pl.ds(pl.multiple_of(c * 128, 128), 128)]
        for j in range(slots):
            tile_ids[j] = jnp.broadcast_to(ids[j : j + 1, :], (16, 128))
            tile_tw[j] = jnp.broadcast_to(tw[j : j + 1, :], (16, 128))

        def band(r, carry):
            shape = (15, 16, 128)
            term_of = (
                lax.broadcasted_iota(jnp.int32, shape, 0) * 16 + lax.broadcasted_iota(jnp.int32, shape, 1) + r * 240
            ).astype(jnp.int16)
            acc = jnp.zeros(shape, jnp.bfloat16)
            for j in range(slots):
                acc = jnp.where(tile_ids[j][None] == term_of, tile_tw[j][None], acc)
            dense[c, pl.ds(pl.multiple_of(r * 240, 240), 240), :] = acc.reshape(240, 128)
            return carry

        lax.fori_loop(0, width // 240, band, 0)
        if k == 0:
            local[4].wait()
        share = lax.dot_general(
            dense[c], slab_v[...], (((0,), (0,)), ((), ())), preferred_element_type=jnp.float32
        )
        for d in range(NX):
            part[c, d, :, 384:512] = jnp.zeros((32, 128), jnp.float32)
            part[c, d, :, 0:stored] = share[d * 32 : (d + 1) * 32, :]

    chunk(0)
    local[2].wait()
    local[3].wait()
    pl.semaphore_wait(barrier, near + 8)

    def half(owner, o, h):
        return feats.at[owner, o, pl.ds(h * 16, 16)]

    def z_send(o, way, hop, h):
        to = zl + hop if way == 0 else zl - hop
        return remote(half(x, o, h), half(x, o, h), zs.at[way, o, hop // 2, h], zr.at[o, h], term=at_zl(to))

    def z_onward(o, k, way, h, finish=False):
        for hop in ONWARD.get(k, ()):
            @pl.when(zl + hop < NZ if way == 0 else zl >= hop)
            def _():
                copy = z_send(o, way, hop, h)
                copy.wait_send() if finish else copy.start()

    def x_send(o, way, h):
        return remote(half(x, o, h), half(x, o, h), xs.at[way, o, h], xr.at[way, o, h], term=at_x((1, 3)[way]))

    def x_forward(o, way):
        rows = half(lax.rem(x + (3, 1)[way], NX), o, way)
        return remote(rows, rows, hs.at[way, o], hr.at[way, o], term=at_x((1, 3)[way]))

    def x_take(o, way, h):
        rows = half(lax.rem(x + (3, 1)[way], NX), o, h)
        remote(rows, rows, xs.at[way, o, h], xr.at[way, o, h], term=at_x((1, 3)[way])).wait_recv()

    def half_take(o, way):
        rows = half(lax.rem(x + 2, NX), o, way)
        remote(rows, rows, hs.at[way, o], hr.at[way, o], term=at_x((1, 3)[way])).wait_recv()

    def sides(k, act):
        @pl.when(zl >= k)
        def _():
            act(zl - k, 0)

        @pl.when(zl + k < NZ)
        def _():
            act(zl + k, 1)

    def arrive(k):
        def act(o, way):
            for h in (0, 1):
                z_send(o, way, 1, h).wait_recv()
                z_onward(o, k, way, h)
                x_send(o, h, h).start()
                x_send(o, 1 - h, h).start()

        sides(k, act)

    def pass_on(k):
        def act(o, way):
            for turn in (0, 1):
                x_take(o, turn, turn)
                x_forward(o, turn).start()

        act(zl, 0) if k == 0 else sides(k, act)

    def rows_of(h, yy, cc, lo=0, n=64):
        return weight.at[pl.ds(pl.multiple_of((h * 8 + yy * 2 + cc) * 64 + lo, 32), n)]

    def relay_send(way):
        return remote(rows_of(zh, y, core, way * 32, 32), relay.at[way], rs.at[way], rr.at[way], **at_z((4, 12)[way]))

    def relay_on(way):
        far = at_z((4, 12)[way])
        h = lax.div(far["img"], 8)
        dst = rows_of(1 - h, y, core, way * 32, 32)
        return remote(relay.at[way], dst, ws.at[way], wr.at[way], **far)

    def relay_take(way):
        far = at_z((4, 12)[way])
        dst = rows_of(1 - zh, y, core, way * 32, 32)
        remote(relay.at[way], dst, ws.at[way], wr.at[way], **far).wait_recv()

    def y_send(b, d):
        rows = rows_of(zh if b == 0 else 1 - zh, y, core)
        return remote(rows, rows, ys.at[b, d - 1], yr.at[b, d - 1], img=at_y(d))

    def y_take(b, d):
        h = zh if b == 0 else 1 - zh
        dst = rows_of(h, lax.rem(y + NY - d, NY), core)
        remote(dst, dst, ys.at[b, d - 1], yr.at[b, d - 1], img=at_y(d)).wait_recv()

    def c_send(b, d):
        h = zh if b == 0 else 1 - zh
        rows = rows_of(h, lax.rem(y + NY - d, NY), core)
        return remote(rows, rows, cs.at[b, d], cr.at[b, d], img=partner)

    def c_take(b, d):
        h = zh if b == 0 else 1 - zh
        dst = rows_of(h, lax.rem(y + NY - d, NY), 1 - core)
        remote(dst, dst, cs.at[b, d], cr.at[b, d], img=partner).wait_recv()

    pos = lax.broadcasted_iota(jnp.int32, (32, 512), 1)

    def encode(v):
        v = jnp.where(pos < stored, v, 0.0)
        top = jnp.max(v, axis=1, keepdims=True)
        power = jnp.ceil(jnp.log2(jnp.maximum(top, 2.0**-100)))
        code = jnp.minimum((v * (jnp.exp2(-power) * 65535.0) + 0.5).astype(jnp.int32), 65535) - 32768
        return jnp.where(pos == stored, power.astype(jnp.int32), code).astype(jnp.int16)

    def decode(code):
        code = code.astype(jnp.int32)
        step = jnp.exp2(code[:, stored : stored + 1].astype(jnp.float32)) * (1.0 / 65535.0)
        return (code + 32768).astype(jnp.float32) * step

    def share_copy(k, d):
        return remote(x_out.at[k, d - 1], x_in.at[k, d - 1], as_.at[k, d - 1], ar.at[k, d - 1], term=at_x(d))

    def q_copy(k):
        c = lax.rem(zl + FAR[k], NZ)
        return remote(z_out.at[k], z_in.at[k], qs.at[k], qr.at[k], term=at_zl(c))

    def shares(k):
        c = lax.rem(zl + FAR[k], NZ)
        for d in (2, 1, 3):
            x_out[k, d - 1] = encode(part[c, lax.rem(x + d, NX)])
            share_copy(k, d).start()

    def gather_shares(k):
        c = lax.rem(zl + FAR[k], NZ)
        total = part[c, x]
        for d in range(1, NX):
            share_copy(k, d).wait_recv()
            total = total + decode(x_in[k, d - 1])
        if FAR[k]:
            z_out[k] = encode(total)
            q_copy(k).start()
        else:
            part[c, x] = total

    for way in (0, 1):
        relay_send(way).start()
    for h in (0, 1):
        for way in (0, 1):
            z_onward(zl, 0, way, h)
    for h in (0, 1):
        x_send(zl, h, h).start()
        x_send(zl, 1 - h, h).start()
    for d in range(1, NY):
        y_send(0, d).start()
    c_send(0, 0).start()

    def relayed():
        for way in (0, 1):
            relay_send(way).wait_recv()
            relay_on(way).start()

    def other_half():
        for way in (0, 1):
            relay_take(way)
        for d in range(1, NY):
            y_send(1, d).start()
        c_send(1, 0).start()

    def to_partner(b, d):
        y_take(b, d)
        c_send(b, d).start()

    def project(d):
        for o in range(NZ):
            if d == 2:
                half_take(o, 0)
                half_take(o, 1)
            elif d == 3:
                x_take(o, 0, 1)
            elif d == 1:
                x_take(o, 1, 0)
        rows = feats[lax.rem(x + d, NX)].reshape(NZ * 32, feats.shape[3])
        logits = jnp.dot(rows, weight[...], preferred_element_type=jnp.float32)
        best = jnp.max(logits.reshape(NZ, 32, width), axis=0)
        runmax[...] = best if d == 0 else jnp.maximum(runmax[...], best)

    def impacts():
        best = jnp.max(runmax[...].reshape(4, 8, width), axis=1)
        best = jnp.log1p(jnp.maximum(best + bias_ref[...], 0.0)).astype(jnp.bfloat16)
        best = jnp.concatenate([best, jnp.zeros_like(best)], axis=0)
        for k in range(NZ):
            fresh[k] = jnp.dot(best, dense[k], preferred_element_type=jnp.float32)
        for d in range(1, NX):
            tx_copy(d).start()

    def tx_copy(d):
        return remote(fresh, fresh_x.at[d - 1], tx_s.at[d - 1], tx_r.at[d - 1], term=at_x(d))

    def tz_copy(d):
        to = lax.rem(zl + d, NZ)
        return remote(fresh_z.at[to], fresh_in.at[d - 1], tz_s.at[d - 1], tz_r.at[d - 1], term=at_zl(to))

    def out_along_z():
        for d in range(1, NX):
            tx_copy(d).wait_recv()
        fresh_z[...] = fresh[...] + (fresh_x[0] + fresh_x[1] + fresh_x[2])
        for d in range(1, NZ):
            tz_copy(d).start()

    def rows_there():
        for b in (0, 1):
            for d in range(NY):
                c_take(b, d)

    acts = {
        "arrive": arrive, "pass": pass_on, "relay": relayed, "other": other_half,
        "row": lambda d: to_partner(0, d), "row2": lambda d: to_partner(1, d),
        "chunk": chunk, "shares": shares, "gather": gather_shares, "rows": rows_there, "project": project,
        "new": impacts, "new2": out_along_z,
    }
    for name, *at in PLAN:
        acts[name](*at)
    for k in ONWARD:
        for h in (0, 1):
            if k == 0:
                z_onward(zl, 0, 0, h, True)
                z_onward(zl, 0, 1, h, True)
            else:
                sides(k, lambda o, way: z_onward(o, k, way, h, True))
    for o in range(NZ):
        for way in (0, 1):
            x_send(o, way, 0).wait_send()
            x_send(o, way, 1).wait_send()
            x_forward(o, way).wait_send()
    for way in (0, 1):
        relay_send(way).wait_send()
        relay_on(way).wait_send()
    for b in (0, 1):
        for d in range(1, NY):
            y_send(b, d).wait_send()
        for d in range(NY):
            c_send(b, d).wait_send()
    for k in range(NZ):
        for d in range(1, NX):
            share_copy(k, d).wait_send()
        if FAR[k]:
            q_copy(k).wait_send()
    for d in range(1, NX):
        tx_copy(d).wait_send()
    for d in range(1, NZ):
        tz_copy(d).wait_send()

    result = part[zl, x]
    for k in range(NZ - 1):
        q_copy(k).wait_recv()
        result = result + decode(z_in[k])
    out_ref[...] = result

    total = fresh_z[zl]
    for d in range(1, NZ):
        tz_copy(d).wait_recv()
        total = total + fresh_in[d - 1]
    turned[...] = jnp.concatenate([total, jnp.zeros((120, 128), jnp.float32)], axis=0).T
    mine = pltpu.roll(turned[pl.ds(pl.multiple_of(x * 32, 32), 32), :], stored % 128, 1)
    lane = lax.broadcasted_iota(jnp.int32, (32, 128), 1)
    last = out_ref[:, 384:512]
    out_ref[:, 384:512] = jnp.where(lane >= stored % 128, mine, last)


def shards(patches, patch_mask, proj_weight, proj_bias, slab, query_ids, term_weights):
    images, chunk, depth = patches.shape
    rows = images * chunk
    width = proj_weight.shape[1]
    queries, slots = query_ids.shape
    stored = slab.shape[0]
    f32, b16, i16 = jnp.float32, jnp.bfloat16, jnp.int16
    dma = pltpu.SemaphoreType.DMA
    vmem = pl.BlockSpec(memory_space=pltpu.VMEM)
    hbm = pl.BlockSpec(memory_space=pl.ANY)
    return pl.pallas_call(
        kernel,
        out_shape=jax.ShapeDtypeStruct((32, 512), f32),
        in_specs=[hbm, hbm, vmem, vmem, hbm, hbm, hbm],
        out_specs=vmem,
        scratch_shapes=[
            pltpu.VMEM((slots, queries), jnp.int32),
            pltpu.VMEM((slots, queries), b16),
            pltpu.VMEM((width, stored), b16),
            pltpu.VMEM((slots, 16, 128), i16),
            pltpu.VMEM((slots, 16, 128), b16),
            pltpu.VMEM((NX, NZ, rows, depth + EXTRA), b16),
            pltpu.VMEM((depth + EXTRA, width), b16),
            pltpu.VMEM((NZ, width, 128), b16),
            pltpu.VMEM((NZ, NX, 32, 512), f32),
            pltpu.VMEM((NZ, NX - 1, 32, 512), i16),
            pltpu.VMEM((NZ, NX - 1, 32, 512), i16),
            pltpu.VMEM((NZ - 1, 32, 512), i16),
            pltpu.VMEM((NZ - 1, 32, 512), i16),
            pltpu.VMEM((2, 32, width), b16),
            pltpu.VMEM((rows, width), f32),
            pltpu.VMEM((NZ, 8, 128), f32),
            pltpu.VMEM((NX - 1, NZ, 8, 128), f32),
            pltpu.VMEM((NZ, 8, 128), f32),
            pltpu.VMEM((NZ - 1, 8, 128), f32),
            pltpu.VMEM((128, 128), f32),
            dma((5,)),
            dma((2, NZ, 3, 2)), dma((NZ, 2)), dma((2, NZ, 2)), dma((2, NZ, 2)), dma((2, NZ)), dma((2, NZ)),
            dma((2,)), dma((2,)), dma((2,)), dma((2,)),
            dma((2, NY - 1)), dma((2, NY - 1)), dma((2, NY)), dma((2, NY)),
            dma((NZ, NX - 1)), dma((NZ, NX - 1)), dma((NZ - 1,)), dma((NZ - 1,)),
            dma((NX - 1,)), dma((NX - 1,)), dma((NZ - 1,)), dma((NZ - 1,)),
        ],
        compiler_params=pltpu.CompilerParams(
            collective_id=0, has_side_effects=True, vmem_limit_bytes=60 * 1024 * 1024
        ),
        name="score",
    )(
        query_ids.T, term_weights.T, patch_mask, proj_bias.reshape(1, width), patches.reshape(rows, depth),
        proj_weight, slab.T,
    )


def solution(mesh):
    placed = (
        P("img", "term", None),
        P("img", "term"),
        P("img", "term"),
        P("term"),
        P("img", "term"),
        P(),
        P(),
    )
    return jax.shard_map(
        shards, mesh=mesh, in_specs=placed, out_specs=P("term", "img"), check_vma=False
    )
```

```python
import functools

import jax
import jax.numpy as jnp
from jax import lax
from jax.experimental import pallas as pl
from jax.experimental.pallas import tpu as pltpu
from jax.sharding import PartitionSpec as P

MESH = pl.DeviceIdType.MESH
NX, NY, NZ, NH = 4, 4, 8, 2
FAR = (4, 3, 5, 2, 6, 1, 7, 0)
ONWARD = {0: (1,), 1: (1,), 2: (1,), 3: (1,), 4: (1,), 5: (1,), 6: (1,)}
MASKED = -1e30
PADDING = 64.0
PLAN = (
    ("chunk", 1), ("shares", 0), ("chunk", 2), ("shares", 1), ("chunk", 3), ("shares", 2), ("chunk", 4),
    ("shares", 3), ("arrive", 1), ("relay",), ("pass", 0), ("chunk", 5), ("shares", 4), ("arrive", 2),
    ("chunk", 6), ("shares", 5), ("pass", 1), ("arrive", 3), ("chunk", 7), ("shares", 6), ("shares", 7),
    ("pass", 2), ("arrive", 4), ("other",), ("row", 1), ("row", 2), ("row", 3), ("arrive", 5), ("pass", 3),
    ("arrive", 6), ("pass", 4), ("arrive", 7), ("pass", 5), ("row2", 1), ("row2", 2), ("row2", 3),
    ("pass", 6), ("gather", 0), ("gather", 1), ("pass", 7), ("gather", 2), ("rows",), ("project", 0),
    ("project", 1), ("gather", 3), ("project", 3), ("project", 2), ("new",), ("gather", 4), ("gather", 5),
    ("new2",), ("gather", 6), ("gather", 7),
)


def remote(src, dst, send, recv, **where):
    return pltpu.make_async_remote_copy(
        src_ref=src, dst_ref=dst, send_sem=send, recv_sem=recv, device_id=where, device_id_type=MESH
    )


def kernel(
    ids_ref, tw_ref, mask_ref, bias_ref, pat_ref, wt_ref, slab_ref,
    out_ref,
    ids_v, tw_v, slab_v, tile_ids, tile_tw, feats, weight, dense, part, x_out, x_in, z_out, z_in, relay, runmax,
    fresh, fresh_x, fresh_z, fresh_in, turned,
    ls, zs, zr, xs, xr, hs, hr, rs, rr, ws, wr, ys, yr, cs, cr,
    as_, ar, qs, qr, tx_s, tx_r, tz_s, tz_r,
):
    img = lax.axis_index("img")
    term = lax.axis_index("term")
    core, y, zh = lax.rem(img, 2), lax.rem(lax.div(img, 2), NY), lax.div(img, 2 * NY)
    x, zl = lax.rem(term, NX), lax.div(term, NX)
    width = weight.shape[1]
    stored = slab_v.shape[1]

    def at_x(d):
        return zl * NX + lax.rem(x + d, NX)

    def at_zl(k):
        return k * NX + x

    def at_y(d):
        return zh * 8 + lax.rem(y + d, NY) * 2 + core

    def at_z(d):
        far = lax.rem(zh * NZ + zl + d, NH * NZ)
        return {"img": lax.div(far, NZ) * 8 + y * 2 + core, "term": lax.rem(far, NZ) * NX + x}

    partner = zh * 8 + y * 2 + 1 - core

    barrier = pltpu.get_barrier_semaphore()
    for hop in (4, 2, 1):
        for to in (zl + hop, zl - hop):
            @pl.when(jnp.logical_and(to >= 0, to < NZ))
            def _():
                pl.semaphore_signal(barrier, inc=1, device_id={"term": at_zl(to)}, device_id_type=MESH)
    pl.semaphore_signal(barrier, inc=1, device_id=at_z(jnp.where(zl < 4, 12, 4)), device_id_type=MESH)
    for d in range(1, NX):
        pl.semaphore_signal(barrier, inc=1, device_id={"term": at_x(d)}, device_id_type=MESH)
    for d in range(1, NY):
        pl.semaphore_signal(barrier, inc=1, device_id={"img": at_y(d)}, device_id_type=MESH)
    pl.semaphore_signal(barrier, inc=1, device_id={"img": partner}, device_id_type=MESH)
    near = 1 + jnp.where(jnp.logical_or(zl == 0, zl == NZ - 1), 1, 2) + jnp.where(
        jnp.logical_or(zl < 2, zl >= NZ - 2), 1, 2
    )

    own = weight.at[pl.ds(pl.multiple_of(img * 64, 64), 64)]
    local = [
        pltpu.make_async_copy(ids_ref, ids_v, ls.at[0]),
        pltpu.make_async_copy(tw_ref, tw_v, ls.at[1]),
        pltpu.make_async_copy(pat_ref, feats.at[x, zl], ls.at[2]),
        pltpu.make_async_copy(wt_ref, own, ls.at[3]),
        pltpu.make_async_copy(slab_ref, slab_v, ls.at[4]),
    ]
    for copy in local:
        copy.start()

    square = lax.broadcasted_iota(jnp.int32, (8, 8), 0) == lax.broadcasted_iota(jnp.int32, (8, 8), 1)
    off = []
    for n in range(mask_ref.shape[0]):
        row = jnp.broadcast_to(mask_ref[n : n + 1, :], (8, 8)).astype(jnp.float32)
        off.append(1.0 - jnp.sum(jnp.where(square, row, 0.0), axis=1, keepdims=True))
    off = jnp.concatenate(off, axis=0)

    first = term * width
    local[0].wait()
    local[1].wait()

    def chunk(k):
        c = lax.rem(zl + FAR[k], NZ)
        slots = ids_v.shape[0]
        ids = (ids_v[:, pl.ds(pl.multiple_of(c * 128, 128), 128)] - first).astype(jnp.int16)
        tw = tw_v[:, pl.ds(pl.multiple_of(c * 128, 128), 128)]
        for j in range(slots):
            tile_ids[j] = jnp.broadcast_to(ids[j : j + 1, :], (16, 128))
            tile_tw[j] = jnp.broadcast_to(tw[j : j + 1, :], (16, 128))

        def band(r, carry):
            shape = (15, 16, 128)
            term_of = (
                lax.broadcasted_iota(jnp.int32, shape, 0) * 16 + lax.broadcasted_iota(jnp.int32, shape, 1) + r * 240
            ).astype(jnp.int16)
            acc = jnp.zeros(shape, jnp.bfloat16)
            for j in range(slots):
                acc = jnp.where(tile_ids[j][None] == term_of, tile_tw[j][None], acc)
            dense[c, pl.ds(pl.multiple_of(r * 240, 240), 240), :] = acc.reshape(240, 128)
            return carry

        lax.fori_loop(0, width // 240, band, 0)
        if k == 0:
            local[4].wait()
        share = lax.dot_general(
            dense[c], slab_v[...], (((0,), (0,)), ((), ())), preferred_element_type=jnp.float32
        )
        for d in range(NX):
            part[c, d, :, 384:512] = jnp.zeros((32, 128), jnp.float32)
            part[c, d, :, 0:stored] = share[d * 32 : (d + 1) * 32, :]

    chunk(0)
    local[2].wait()
    feats[x, zl] = jnp.where(off > 0.5, PADDING, feats[x, zl].astype(jnp.float32)).astype(jnp.bfloat16)
    local[3].wait()
    pl.semaphore_wait(barrier, near + 8)

    def half(owner, o, h):
        return feats.at[owner, o, pl.ds(h * 16, 16)]

    def z_send(o, way, hop, h):
        to = zl + hop if way == 0 else zl - hop
        return remote(half(x, o, h), half(x, o, h), zs.at[way, o, hop // 2, h], zr.at[o, h], term=at_zl(to))

    def z_onward(o, k, way, h, finish=False):
        for hop in ONWARD.get(k, ()):
            @pl.when(zl + hop < NZ if way == 0 else zl >= hop)
            def _():
                copy = z_send(o, way, hop, h)
                copy.wait_send() if finish else copy.start()

    def x_send(o, way, h):
        return remote(half(x, o, h), half(x, o, h), xs.at[way, o, h], xr.at[way, o, h], term=at_x((1, 3)[way]))

    def x_forward(o, way):
        rows = half(lax.rem(x + (3, 1)[way], NX), o, way)
        return remote(rows, rows, hs.at[way, o], hr.at[way, o], term=at_x((1, 3)[way]))

    def x_take(o, way, h):
        rows = half(lax.rem(x + (3, 1)[way], NX), o, h)
        remote(rows, rows, xs.at[way, o, h], xr.at[way, o, h], term=at_x((1, 3)[way])).wait_recv()

    def half_take(o, way):
        rows = half(lax.rem(x + 2, NX), o, way)
        remote(rows, rows, hs.at[way, o], hr.at[way, o], term=at_x((1, 3)[way])).wait_recv()

    def sides(k, act):
        @pl.when(zl >= k)
        def _():
            act(zl - k, 0)

        @pl.when(zl + k < NZ)
        def _():
            act(zl + k, 1)

    def arrive(k):
        def act(o, way):
            for h in (0, 1):
                z_send(o, way, 1, h).wait_recv()
                z_onward(o, k, way, h)
                x_send(o, h, h).start()
                x_send(o, 1 - h, h).start()

        sides(k, act)

    def pass_on(k):
        def act(o, way):
            for turn in (0, 1):
                x_take(o, turn, turn)
                x_forward(o, turn).start()

        act(zl, 0) if k == 0 else sides(k, act)

    def rows_of(h, yy, cc, lo=0, n=64):
        return weight.at[pl.ds(pl.multiple_of((h * 8 + yy * 2 + cc) * 64 + lo, 32), n)]

    def relay_send(way):
        return remote(rows_of(zh, y, core, way * 32, 32), relay.at[way], rs.at[way], rr.at[way], **at_z((4, 12)[way]))

    def relay_on(way):
        far = at_z((4, 12)[way])
        h = lax.div(far["img"], 8)
        dst = rows_of(1 - h, y, core, way * 32, 32)
        return remote(relay.at[way], dst, ws.at[way], wr.at[way], **far)

    def relay_take(way):
        far = at_z((4, 12)[way])
        dst = rows_of(1 - zh, y, core, way * 32, 32)
        remote(relay.at[way], dst, ws.at[way], wr.at[way], **far).wait_recv()

    def y_send(b, d):
        rows = rows_of(zh if b == 0 else 1 - zh, y, core)
        return remote(rows, rows, ys.at[b, d - 1], yr.at[b, d - 1], img=at_y(d))

    def y_take(b, d):
        h = zh if b == 0 else 1 - zh
        dst = rows_of(h, lax.rem(y + NY - d, NY), core)
        remote(dst, dst, ys.at[b, d - 1], yr.at[b, d - 1], img=at_y(d)).wait_recv()

    def c_send(b, d):
        h = zh if b == 0 else 1 - zh
        rows = rows_of(h, lax.rem(y + NY - d, NY), core)
        return remote(rows, rows, cs.at[b, d], cr.at[b, d], img=partner)

    def c_take(b, d):
        h = zh if b == 0 else 1 - zh
        dst = rows_of(h, lax.rem(y + NY - d, NY), 1 - core)
        remote(dst, dst, cs.at[b, d], cr.at[b, d], img=partner).wait_recv()

    pos = lax.broadcasted_iota(jnp.int32, (32, 512), 1)

    def encode(v):
        v = jnp.where(pos < stored, v, 0.0)
        top = jnp.max(v, axis=1, keepdims=True)
        power = jnp.ceil(jnp.log2(jnp.maximum(top, 2.0**-100)))
        code = jnp.minimum((v * (jnp.exp2(-power) * 65535.0) + 0.5).astype(jnp.int32), 65535) - 32768
        return jnp.where(pos == stored, power.astype(jnp.int32), code).astype(jnp.int16)

    def decode(code):
        code = code.astype(jnp.int32)
        step = jnp.exp2(code[:, stored : stored + 1].astype(jnp.float32)) * (1.0 / 65535.0)
        return (code + 32768).astype(jnp.float32) * step

    def share_copy(k, d):
        return remote(x_out.at[k, d - 1], x_in.at[k, d - 1], as_.at[k, d - 1], ar.at[k, d - 1], term=at_x(d))

    def q_copy(k):
        c = lax.rem(zl + FAR[k], NZ)
        return remote(z_out.at[k], z_in.at[k], qs.at[k], qr.at[k], term=at_zl(c))

    def shares(k):
        c = lax.rem(zl + FAR[k], NZ)
        for d in (2, 1, 3):
            x_out[k, d - 1] = encode(part[c, lax.rem(x + d, NX)])
            share_copy(k, d).start()

    def gather_shares(k):
        c = lax.rem(zl + FAR[k], NZ)
        total = part[c, x]
        for d in range(1, NX):
            share_copy(k, d).wait_recv()
            total = total + decode(x_in[k, d - 1])
        if FAR[k]:
            z_out[k] = encode(total)
            q_copy(k).start()
        else:
            part[c, x] = total

    for way in (0, 1):
        relay_send(way).start()
    for h in (0, 1):
        for way in (0, 1):
            z_onward(zl, 0, way, h)
    for h in (0, 1):
        x_send(zl, h, h).start()
        x_send(zl, 1 - h, h).start()
    for d in range(1, NY):
        y_send(0, d).start()
    c_send(0, 0).start()

    def relayed():
        for way in (0, 1):
            relay_send(way).wait_recv()
            relay_on(way).start()

    def other_half():
        for way in (0, 1):
            relay_take(way)
        for d in range(1, NY):
            y_send(1, d).start()
        c_send(1, 0).start()

    def to_partner(b, d):
        y_take(b, d)
        c_send(b, d).start()

    def project(d):
        for o in range(NZ):
            if d == 2:
                half_take(o, 0)
                half_take(o, 1)
            elif d == 3:
                x_take(o, 0, 1)
            elif d == 1:
                x_take(o, 1, 0)
        rows = feats[lax.rem(x + d, NX)].reshape(NZ * 32, feats.shape[3])
        logits = jnp.dot(rows, weight[...], preferred_element_type=jnp.float32)
        padding = rows[:, 0:128].astype(jnp.float32)[:, 0:1] > 0.5 * PADDING
        logits = logits + jnp.where(padding, MASKED, 0.0)
        best = jnp.max(logits.reshape(NZ, 32, width), axis=0)
        runmax[...] = best if d == 0 else jnp.maximum(runmax[...], best)

    def impacts():
        best = jnp.max(runmax[...].reshape(4, 8, width), axis=1)
        best = jnp.log1p(jnp.maximum(best + bias_ref[...], 0.0)).astype(jnp.bfloat16)
        best = jnp.concatenate([best, jnp.zeros_like(best)], axis=0)
        for k in range(NZ):
            fresh[k] = jnp.dot(best, dense[k], preferred_element_type=jnp.float32)
        for d in range(1, NX):
            tx_copy(d).start()

    def tx_copy(d):
        return remote(fresh, fresh_x.at[d - 1], tx_s.at[d - 1], tx_r.at[d - 1], term=at_x(d))

    def tz_copy(d):
        to = lax.rem(zl + d, NZ)
        return remote(fresh_z.at[to], fresh_in.at[d - 1], tz_s.at[d - 1], tz_r.at[d - 1], term=at_zl(to))

    def out_along_z():
        for d in range(1, NX):
            tx_copy(d).wait_recv()
        fresh_z[...] = fresh[...] + (fresh_x[0] + fresh_x[1] + fresh_x[2])
        for d in range(1, NZ):
            tz_copy(d).start()

    def rows_there():
        for b in (0, 1):
            for d in range(NY):
                c_take(b, d)

    acts = {
        "arrive": arrive, "pass": pass_on, "relay": relayed, "other": other_half,
        "row": lambda d: to_partner(0, d), "row2": lambda d: to_partner(1, d),
        "chunk": chunk, "shares": shares, "gather": gather_shares, "rows": rows_there, "project": project,
        "new": impacts, "new2": out_along_z,
    }
    for name, *at in PLAN:
        acts[name](*at)
    for k in ONWARD:
        for h in (0, 1):
            if k == 0:
                z_onward(zl, 0, 0, h, True)
                z_onward(zl, 0, 1, h, True)
            else:
                sides(k, lambda o, way: z_onward(o, k, way, h, True))
    for o in range(NZ):
        for way in (0, 1):
            x_send(o, way, 0).wait_send()
            x_send(o, way, 1).wait_send()
            x_forward(o, way).wait_send()
    for way in (0, 1):
        relay_send(way).wait_send()
        relay_on(way).wait_send()
    for b in (0, 1):
        for d in range(1, NY):
            y_send(b, d).wait_send()
        for d in range(NY):
            c_send(b, d).wait_send()
    for k in range(NZ):
        for d in range(1, NX):
            share_copy(k, d).wait_send()
        if FAR[k]:
            q_copy(k).wait_send()
    for d in range(1, NX):
        tx_copy(d).wait_send()
    for d in range(1, NZ):
        tz_copy(d).wait_send()

    result = part[zl, x]
    for k in range(NZ - 1):
        q_copy(k).wait_recv()
        result = result + decode(z_in[k])
    out_ref[...] = result

    total = fresh_z[zl]
    for d in range(1, NZ):
        tz_copy(d).wait_recv()
        total = total + fresh_in[d - 1]
    turned[...] = jnp.concatenate([total, jnp.zeros((120, 128), jnp.float32)], axis=0).T
    mine = pltpu.roll(turned[pl.ds(pl.multiple_of(x * 32, 32), 32), :], stored % 128, 1)
    lane = lax.broadcasted_iota(jnp.int32, (32, 128), 1)
    last = out_ref[:, 384:512]
    out_ref[:, 384:512] = jnp.where(lane >= stored % 128, mine, last)


def shards(patches, patch_mask, proj_weight, proj_bias, slab, query_ids, term_weights):
    images, chunk, depth = patches.shape
    rows = images * chunk
    width = proj_weight.shape[1]
    queries, slots = query_ids.shape
    stored = slab.shape[0]
    f32, b16, i16 = jnp.float32, jnp.bfloat16, jnp.int16
    dma = pltpu.SemaphoreType.DMA
    vmem = pl.BlockSpec(memory_space=pltpu.VMEM)
    hbm = pl.BlockSpec(memory_space=pl.ANY)
    return pl.pallas_call(
        kernel,
        out_shape=jax.ShapeDtypeStruct((32, 512), f32),
        in_specs=[hbm, hbm, vmem, vmem, hbm, hbm, hbm],
        out_specs=vmem,
        scratch_shapes=[
            pltpu.VMEM((slots, queries), jnp.int32),
            pltpu.VMEM((slots, queries), b16),
            pltpu.VMEM((width, stored), b16),
            pltpu.VMEM((slots, 16, 128), i16),
            pltpu.VMEM((slots, 16, 128), b16),
            pltpu.VMEM((NX, NZ, rows, depth), b16),
            pltpu.VMEM((depth, width), b16),
            pltpu.VMEM((NZ, width, 128), b16),
            pltpu.VMEM((NZ, NX, 32, 512), f32),
            pltpu.VMEM((NZ, NX - 1, 32, 512), i16),
            pltpu.VMEM((NZ, NX - 1, 32, 512), i16),
            pltpu.VMEM((NZ - 1, 32, 512), i16),
            pltpu.VMEM((NZ - 1, 32, 512), i16),
            pltpu.VMEM((2, 32, width), b16),
            pltpu.VMEM((rows, width), f32),
            pltpu.VMEM((NZ, 8, 128), f32),
            pltpu.VMEM((NX - 1, NZ, 8, 128), f32),
            pltpu.VMEM((NZ, 8, 128), f32),
            pltpu.VMEM((NZ - 1, 8, 128), f32),
            pltpu.VMEM((128, 128), f32),
            dma((5,)),
            dma((2, NZ, 3, 2)), dma((NZ, 2)), dma((2, NZ, 2)), dma((2, NZ, 2)), dma((2, NZ)), dma((2, NZ)),
            dma((2,)), dma((2,)), dma((2,)), dma((2,)),
            dma((2, NY - 1)), dma((2, NY - 1)), dma((2, NY)), dma((2, NY)),
            dma((NZ, NX - 1)), dma((NZ, NX - 1)), dma((NZ - 1,)), dma((NZ - 1,)),
            dma((NX - 1,)), dma((NX - 1,)), dma((NZ - 1,)), dma((NZ - 1,)),
        ],
        compiler_params=pltpu.CompilerParams(
            collective_id=0, has_side_effects=True, vmem_limit_bytes=60 * 1024 * 1024
        ),
        name="score",
    )(
        query_ids.T, term_weights.T, patch_mask, proj_bias.reshape(1, width), patches.reshape(rows, depth),
        proj_weight, slab.T,
    )


def solution(mesh):
    placed = (
        P("img", "term", None),
        P("img", "term"),
        P("img", "term"),
        P("term"),
        P("img", "term"),
        P(),
        P(),
    )
    return jax.shard_map(
        shards, mesh=mesh, in_specs=placed, out_specs=P("term", "img"), check_vma=False
    )
```
